256 devices in a mesh: section: 4 (over y), orient: 64 (over z, x, core).
Axes of the slice: x: 4, y: 4, z: 8, core: 2. Of those that a mesh axis runs over, the one named last changes fastest.
Arguments:
- patterns: bfloat16 [4, 128, 65536], P('section', None, 'orient'), may hold values from -6 to 6
- detector_gain: float32 [65536], P('orient'), may hold values from 0.1 to 1.9
- background: float32 [65536], P('orient'), may hold values from -6 to 6
- bin_map: int32 [65536], P('orient'), may hold values from 0 to 12287, as said below
- templates: bfloat16 [102400, 12288], P(('section', 'orient')), may hold values from -0.0546875 to 0.0546875
- best_picks: int32 [4, 128], replicated, may hold values from 0 to 102399
Outputs:
- top_scores: float32 [4, 128, 8], P('section')
- refined: float32 [4, 128, 3], P('section', 'orient')
The draws below stay inside these ranges and needn't reach their ends.
Inputs may be any that keep to these rules, and one draw needn't show every extreme that they name: `bin_map`: each pixel's polar bin r * 192 + a, with r given by the pixel's distance and a by its direction from a beam centre near the middle of the square detector.
All inputs are finite; a program needn't handle non-finite values.
Results may differ from the reference program's by a relative error of at most 0.0065.
Values may be sent and summed in bfloat16 or wider, within the bound.
A program may use at most 256 MiB of HBM per device.

```python
import math
import jax
import jax.numpy as jnp
import numpy as np
from jax import lax

NPIX = 65536
RAD = 64
ANG = 192
TOPK = 8
REACH = 1
PATTERNS = 128
MICRO = 4
TEMPLATES = 102400


def draw_bin_map(key, part):
    side = math.isqrt(NPIX)
    offsets = jax.random.randint(jax.random.fold_in(key, 11), (2,), 0, side // 16 + 1)
    pixel_ids = jnp.arange(NPIX, dtype=jnp.int32)
    across = 2 * (pixel_ids % side) + 1 - side - offsets[0]
    down = 2 * (pixel_ids // side) + 1 - side - offsets[1]
    distance = across * across + down * down
    limit = jnp.max(distance) + 1
    edges = jnp.arange(1, RAD, dtype=jnp.int32)
    radial = jnp.sum((RAD * RAD * distance[:, None] >= edges[None, :] * edges[None, :] * limit).astype(jnp.int32), axis=1)
    angles = 2.0 * np.pi * np.arange(ANG + 1) / ANG
    cos_table = jnp.asarray((4096.0 * np.cos(angles) + 8192.5).astype(np.int32) - 8192)
    sin_table = jnp.asarray((4096.0 * np.sin(angles) + 8192.5).astype(np.int32) - 8192)
    cross = cos_table[None, :] * down[:, None] - sin_table[None, :] * across[:, None]
    inside = (cross[:, :ANG] >= 0) & (cross[:, 1:] < 0)
    sector = jnp.sum(inside.astype(jnp.int32) * jnp.arange(ANG, dtype=jnp.int32)[None, :], axis=1)
    rotated = (sector - sector[0] + 2 * ANG - 1) % ANG
    return (radial * ANG + rotated).astype(jnp.int32)


def set_ends(drawn, key, low, largest):
    longest = drawn.shape.index(max(drawn.shape))
    spots = []
    for shift in (0, 1):
        where = [jax.random.randint(jax.random.fold_in(key, axis), (), 0, length) for axis, length in enumerate(drawn.shape)]
        where[longest] = (where[longest] + shift) % drawn.shape[longest]
        spots.append(tuple(where))
    return drawn.at[spots[0]].set(low).at[spots[1]].set(largest)


def block_levels(key, shape, pieces, least, high):
    level, own = 1.0, jax.random.fold_in(key, 6)
    for axis_at, parts in pieces:
        draws = jnp.exp(jax.random.uniform(jax.random.fold_in(own, axis_at), (parts,), jnp.float32, least / len(pieces), high / len(pieces)))
        level = level * jnp.repeat(draws, shape[axis_at] // parts).reshape([-1 if axis == axis_at else 1 for axis in range(len(shape))])
    return level


def skewed_wide(key, shape, number_of, lean):
    loads = [min(1 << octave, number_of + 1 - (1 << octave)) * (1 << 20) // math.isqrt((1 << octave) ** lean) + 1 for octave in range((number_of + 1).bit_length()) if 1 << octave <= number_of]
    scale = 1 + sum(loads) // (1 << 30)
    table = np.cumsum(np.array([max(1, weight // scale) for weight in loads]))
    pick = jax.random.randint(jax.random.fold_in(key, 1), shape, 0, int(table[len(loads) - 1]))
    start = jnp.left_shift(1, jnp.searchsorted(jnp.asarray(table, jnp.int32), pick, side="right").astype(jnp.int32))
    rank = start - 1 + jax.random.randint(jax.random.fold_in(key, 4), shape, 0, 1 << 30) % jnp.minimum(start, number_of + 1 - start)
    return jax.random.permutation(jax.random.fold_in(key, 2), number_of)[rank].astype(jnp.int32)


def scatter_about(own_key, extent, deviation, bound, cuts=(), held_as=jnp.bfloat16):
    result = jax.random.normal(own_key, extent, jnp.float32) * deviation
    if len(cuts) > 0:
        result = block_levels(own_key, extent, cuts, -0.22, 0.18) * result
    return jnp.clip(result, min=-bound, max=bound).astype(held_as)


def setup_inputs(seed: int = 0) -> dict:
    seeds = jax.random.split(jax.random.key(seed), 7)
    return {
        "patterns": scatter_about(seeds[0], (MICRO, PATTERNS, NPIX), 1.0, 6.0, ((0, 4), (2, 64))),
        "detector_gain": jnp.clip(1.0 + 0.18 * jax.random.normal(seeds[1], (NPIX,), jnp.float32), 0.1, 1.9),
        "background": scatter_about(seeds[2], (NPIX,), 1.0, 6.0, ((0, 64),), jnp.float32),
        "bin_map": draw_bin_map(jax.random.fold_in(seeds[6], 71), 0),
        "templates": scatter_about(seeds[4], (TEMPLATES, RAD * ANG), (RAD * ANG) ** -0.5, 0.0546875, ((0, 256),)),
        "best_picks": set_ends(skewed_wide(seeds[5], (MICRO, PATTERNS), TEMPLATES, 2), jax.random.fold_in(seeds[5], 3), 0, TEMPLATES - 1).astype(jnp.int32),
    }


EPS = 1e-06

def reference(patterns, detector_gain, background, bin_map, templates, best_picks):

    def one_batch(inputs):
        frames, wanted = inputs
        corrected = ((frames.astype(jnp.float32) - background) * detector_gain).astype(jnp.bfloat16)
        bins = jax.ops.segment_sum(corrected.astype(jnp.float32).T, bin_map, num_segments=RAD * ANG)
        squares = lax.optimization_barrier(jnp.sum(bins * bins, axis=0))
        features = (bins * lax.rsqrt(squares / (RAD * ANG) + EPS)).astype(jnp.bfloat16)
        scores = jnp.dot(features.T, templates.T, preferred_element_type=jnp.float32)
        best = lax.top_k(scores, TOPK)[0]
        chosen = jnp.take(templates, wanted, axis=0).reshape(PATTERNS, RAD, ANG).astype(jnp.float32)
        grid = features.reshape(RAD, ANG, PATTERNS).astype(jnp.float32)
        columns = [jnp.einsum('rap,pra->p', grid, jnp.roll(chosen, -offset, axis=2)) for offset in range(-REACH, REACH + 1)]
        return (best, jnp.stack(columns, axis=1))
    best, refined = lax.map(one_batch, (patterns, best_picks))
    return (best, refined)
```

```python
import functools

import jax
import jax.numpy as jnp
from jax import lax
from jax.experimental import pallas as pl
from jax.experimental.pallas import tpu as pltpu
from jax.sharding import PartitionSpec as P

RAD = 64
ANG = 192
TOPK = 8
REACH = 1


EPS = 1e-06
BIN_BLOCK = 1024


def bin_kernel(pat_ref, bg_ref, gain_ref, map_ref, out_ref, corr_ref):
    step = pl.program_id(0)

    @pl.when(step == 0)
    def _():
        corr_ref[...] = (
            (pat_ref[...].astype(jnp.float32) - bg_ref[...]) * gain_ref[...]
        ).astype(jnp.bfloat16)

    height, width = out_ref.shape[0], map_ref.shape[1]
    targets = step * height + lax.broadcasted_iota(jnp.int32, (height, width), 0)
    onehot = (map_ref[...] == targets).astype(jnp.bfloat16)
    out_ref[...] = lax.dot_general(
        onehot, corr_ref[...], (((1,), (1,)), ((), ())), preferred_element_type=jnp.float32
    )


def bin_pixels(frames, background, gain, bin_map, total):
    rows, width = frames.shape
    height = min(BIN_BLOCK, total)
    full = lambda step: (0, 0)
    return pl.pallas_call(
        bin_kernel,
        grid=(total // height,),
        in_specs=[
            pl.BlockSpec((rows, width), full),
            pl.BlockSpec((1, width), full),
            pl.BlockSpec((1, width), full),
            pl.BlockSpec((1, width), full),
        ],
        out_specs=pl.BlockSpec((height, rows), lambda step: (step, 0)),
        out_shape=jax.ShapeDtypeStruct((total, rows), jnp.float32),
        scratch_shapes=[pltpu.VMEM((rows, width), jnp.bfloat16)],
        cost_estimate=pl.CostEstimate(
            flops=2 * total * width * rows, transcendentals=0,
            bytes_accessed=rows * width * 2 + total * rows * 4,
        ),
    )(frames, background[None, :], gain[None, :], bin_map[None, :])


def merge_packed(stack, axis):
    best = jnp.moveaxis(stack[..., :TOPK], axis, -2)
    best = best.reshape(best.shape[:-2] + (best.shape[-2] * TOPK,))
    best = lax.top_k(best, TOPK)[0]
    refined = jnp.sum(stack[..., TOPK:], axis=axis)
    return jnp.concatenate([best, refined], axis=-1)


def body(patterns, detector_gain, background, bin_map, templates, best_picks):
    sections = lax.axis_size("section")
    orients = lax.axis_size("orient")
    section_index = lax.axis_index("section")
    orient_index = lax.axis_index("orient")
    features_total = RAD * ANG
    batches, patterns_per = best_picks.shape
    count = templates.shape[0]

    bins = bin_pixels(patterns[0], background, detector_gain, bin_map, features_total)
    part = lax.psum_scatter(bins, "orient", scatter_dimension=0, tiled=True)
    gathered = lax.all_gather(
        part.astype(jnp.bfloat16), ("section", "orient"), axis=0, tiled=True
    ).reshape(batches, features_total, patterns_per)

    wide = gathered.astype(jnp.float32)
    squares = jnp.sum(wide * wide, axis=1)
    scale = lax.rsqrt(squares / features_total + EPS)

    rings = gathered.reshape(batches, RAD, ANG, patterns_per)
    shifted = [jnp.roll(rings, offset, axis=2) for offset in range(-REACH, REACH + 1)]
    stacked = jnp.stack(shifted, axis=0).reshape(
        2 * REACH + 1, batches, features_total, patterns_per
    )
    raw = lax.dot_general(
        stacked, templates, (((2,), (1,)), ((), ())), preferred_element_type=jnp.float32
    )
    scores = raw[REACH] * scale[:, :, None]
    best = lax.top_k(scores, TOPK)[0]

    group_base = (section_index * orients + orient_index) * count
    local = best_picks - group_base
    owned = local[:, :, None] == lax.broadcasted_iota(jnp.int32, (batches, patterns_per, count), 2)
    picked = jnp.sum(jnp.where(owned[None], raw, 0.0), axis=3) * scale[None]
    packed = jnp.concatenate([best, jnp.moveaxis(picked, 0, -1)], axis=-1)

    mine = lax.all_to_all(packed, "section", 0, 0, tiled=True)
    merged = merge_packed(mine, 0)
    everyone = lax.all_gather(merged, "orient", axis=0)
    final = merge_packed(everyone, 0)
    share = patterns_per // orients
    rows = lax.dynamic_slice_in_dim(final[:, TOPK:], orient_index * share, share, axis=0)
    return (final[None, :, :TOPK], rows[None])


def solution(mesh):
    return jax.shard_map(
        body,
        mesh=mesh,
        in_specs=(
            P("section", None, "orient"),
            P("orient"),
            P("orient"),
            P("orient"),
            P(("section", "orient"), None),
            P(),
        ),
        out_specs=(P("section", None, None), P("section", "orient", None)),
        check_vma=False,
    )
```

```python
import functools

import jax
import jax.numpy as jnp
from jax import lax
from jax.experimental import pallas as pl
from jax.experimental.pallas import tpu as pltpu
from jax.sharding import PartitionSpec as P

RAD = 64
ANG = 192
TOPK = 8
REACH = 1


EPS = 1e-06
BIN_BLOCK = 1024


def bin_kernel(pat_ref, bg_ref, gain_ref, map_ref, out_ref, corr_ref):
    step = pl.program_id(0)

    @pl.when(step == 0)
    def _():
        corr_ref[...] = (
            (pat_ref[...].astype(jnp.float32) - bg_ref[...]) * gain_ref[...]
        ).astype(jnp.bfloat16)

    height, width = out_ref.shape[0], map_ref.shape[1]
    targets = step * height + lax.broadcasted_iota(jnp.int32, (height, width), 0)
    onehot = (map_ref[...] == targets).astype(jnp.bfloat16)
    out_ref[...] = lax.dot_general(
        onehot, corr_ref[...], (((1,), (1,)), ((), ())), preferred_element_type=jnp.float32
    )


def bin_pixels(frames, background, gain, bin_map, total):
    rows, width = frames.shape
    height = min(BIN_BLOCK, total)
    full = lambda step: (0, 0)
    return pl.pallas_call(
        bin_kernel,
        grid=(total // height,),
        in_specs=[
            pl.BlockSpec((rows, width), full),
            pl.BlockSpec((1, width), full),
            pl.BlockSpec((1, width), full),
            pl.BlockSpec((1, width), full),
        ],
        out_specs=pl.BlockSpec((height, rows), lambda step: (step, 0)),
        out_shape=jax.ShapeDtypeStruct((total, rows), jnp.float32),
        scratch_shapes=[pltpu.VMEM((rows, width), jnp.bfloat16)],
        cost_estimate=pl.CostEstimate(
            flops=2 * total * width * rows, transcendentals=0,
            bytes_accessed=rows * width * 2 + total * rows * 4,
        ),
    )(frames, background[None, :], gain[None, :], bin_map[None, :])


def top_values(values):
    width = values.shape[-1]
    place = lax.broadcasted_iota(jnp.int32, values.shape, values.ndim - 1)
    found = []
    for rank in range(TOPK):
        largest = jnp.max(values, axis=-1, keepdims=True)
        found.append(largest)
        if rank + 1 < TOPK:
            first = jnp.min(jnp.where(values == largest, place, width), axis=-1, keepdims=True)
            values = jnp.where(place == first, -jnp.inf, values)
    return jnp.concatenate(found, axis=-1)


def merge_packed(stack, axis):
    best = jnp.moveaxis(stack[..., :TOPK], axis, -2)
    best = best.reshape(best.shape[:-2] + (best.shape[-2] * TOPK,))
    best = top_values(best)
    refined = jnp.sum(stack[..., TOPK:], axis=axis)
    return jnp.concatenate([best, refined], axis=-1)


def body(patterns, detector_gain, background, bin_map, templates, best_picks):
    sections = lax.axis_size("section")
    orients = lax.axis_size("orient")
    section_index = lax.axis_index("section")
    orient_index = lax.axis_index("orient")
    features_total = RAD * ANG
    batches, patterns_per = best_picks.shape
    count = templates.shape[0]

    bins = bin_pixels(patterns[0], background, detector_gain, bin_map, features_total)
    part = lax.psum_scatter(bins.astype(jnp.bfloat16), "orient", scatter_dimension=0, tiled=True)
    gathered = lax.all_gather(
        part, ("section", "orient"), axis=0, tiled=True
    ).reshape(batches, features_total, patterns_per)

    squares = jnp.einsum(
        "mfp,mfp->mp", gathered, gathered, preferred_element_type=jnp.float32
    )
    scale = lax.rsqrt(squares / features_total + EPS)

    slab = templates.reshape(count, RAD, ANG)
    turned = [jnp.roll(slab, -offset, axis=2) for offset in range(-REACH, REACH + 1)]
    rotated = jnp.concatenate(turned, axis=0).reshape((2 * REACH + 1) * count, features_total)
    raw = lax.dot_general(
        gathered, rotated, (((1,), (1,)), ((), ())), preferred_element_type=jnp.float32
    ).reshape(batches, patterns_per, 2 * REACH + 1, count)
    scores = raw[:, :, REACH] * scale[:, :, None]
    best = top_values(scores)

    group_base = (section_index * orients + orient_index) * count
    local = best_picks - group_base
    owned = local[:, :, None] == lax.broadcasted_iota(jnp.int32, (batches, patterns_per, count), 2)
    picked = jnp.sum(jnp.where(owned[:, :, None], raw, 0.0), axis=3) * scale[:, :, None]
    packed = jnp.concatenate([best, picked], axis=-1)

    mine = lax.all_to_all(packed, "section", 0, 0, tiled=True)
    merged = merge_packed(mine, 0)
    everyone = lax.all_gather(merged, "orient", axis=0)
    final = merge_packed(everyone, 0)
    share = patterns_per // orients
    rows = lax.dynamic_slice_in_dim(final[:, TOPK:], orient_index * share, share, axis=0)
    return (final[None, :, :TOPK], rows[None])


def solution(mesh):
    return jax.shard_map(
        body,
        mesh=mesh,
        in_specs=(
            P("section", None, "orient"),
            P("orient"),
            P("orient"),
            P("orient"),
            P(("section", "orient"), None),
            P(),
        ),
        out_specs=(P("section", None, None), P("section", "orient", None)),
        check_vma=False,
    )
```

```python
import functools

import jax
import jax.numpy as jnp
from jax import lax
from jax.experimental import pallas as pl
from jax.experimental.pallas import tpu as pltpu
from jax.sharding import PartitionSpec as P

RAD = 64
ANG = 192
TOPK = 8
REACH = 1


EPS = 1e-06
BIN_BLOCK = 1024


def bin_kernel(pat_ref, bg_ref, gain_ref, map_ref, out_ref, corr_ref):
    step = pl.program_id(0)

    @pl.when(step == 0)
    def _():
        corr_ref[...] = (
            (pat_ref[...].astype(jnp.float32) - bg_ref[...]) * gain_ref[...]
        ).astype(jnp.bfloat16)

    height, width = out_ref.shape[0], map_ref.shape[1]
    targets = step * height + lax.broadcasted_iota(jnp.int32, (height, width), 0)
    onehot = (map_ref[...] == targets).astype(jnp.bfloat16)
    out_ref[...] = lax.dot_general(
        onehot, corr_ref[...], (((1,), (1,)), ((), ())), preferred_element_type=jnp.float32
    )


def bin_pixels(frames, background, gain, bin_map, total):
    rows, width = frames.shape
    height = min(BIN_BLOCK, total)
    full = lambda step: (0, 0)
    return pl.pallas_call(
        bin_kernel,
        grid=(total // height,),
        in_specs=[
            pl.BlockSpec((rows, width), full),
            pl.BlockSpec((1, width), full),
            pl.BlockSpec((1, width), full),
            pl.BlockSpec((1, width), full),
        ],
        out_specs=pl.BlockSpec((height, rows), lambda step: (step, 0)),
        out_shape=jax.ShapeDtypeStruct((total, rows), jnp.float32),
        scratch_shapes=[pltpu.VMEM((rows, width), jnp.bfloat16)],
        cost_estimate=pl.CostEstimate(
            flops=2 * total * width * rows, transcendentals=0,
            bytes_accessed=rows * width * 2 + total * rows * 4,
        ),
    )(frames, background[None, :], gain[None, :], bin_map[None, :])


def top_values(values):
    width = values.shape[-1]
    place = lax.broadcasted_iota(jnp.int32, values.shape, values.ndim - 1)
    found = []
    for rank in range(TOPK):
        largest = jnp.max(values, axis=-1, keepdims=True)
        found.append(largest)
        if rank + 1 < TOPK:
            first = jnp.min(jnp.where(values == largest, place, width), axis=-1, keepdims=True)
            values = jnp.where(place == first, -jnp.inf, values)
    return jnp.concatenate(found, axis=-1)


def merge_packed(stack, axis):
    best = jnp.moveaxis(stack[..., :TOPK], axis, -2)
    best = best.reshape(best.shape[:-2] + (best.shape[-2] * TOPK,))
    best = top_values(best)
    refined = jnp.sum(stack[..., TOPK:], axis=axis)
    return jnp.concatenate([best, refined], axis=-1)


def body(patterns, detector_gain, background, bin_map, templates, best_picks):
    sections = lax.axis_size("section")
    orients = lax.axis_size("orient")
    section_index = lax.axis_index("section")
    orient_index = lax.axis_index("orient")
    features_total = RAD * ANG
    batches, patterns_per = best_picks.shape
    count = templates.shape[0]

    bins = bin_pixels(patterns[0], background, detector_gain, bin_map, features_total)
    pieces = lax.all_to_all(bins.astype(jnp.bfloat16), "orient", 0, 0, tiled=True)
    part = jnp.sum(
        pieces.reshape(orients, features_total // orients, patterns_per).astype(jnp.float32), axis=0
    ).astype(jnp.bfloat16)
    gathered = lax.all_gather(
        part, ("section", "orient"), axis=0, tiled=True
    ).reshape(batches, features_total, patterns_per)

    squares = jnp.einsum(
        "mfp,mfp->mp", gathered, gathered, preferred_element_type=jnp.float32
    )
    scale = lax.rsqrt(squares / features_total + EPS)

    slab = templates.reshape(count, RAD, ANG)
    turned = [jnp.roll(slab, -offset, axis=2) for offset in range(-REACH, REACH + 1)]
    rotated = jnp.concatenate(turned, axis=0).reshape((2 * REACH + 1) * count, features_total)
    raw = lax.dot_general(
        gathered, rotated, (((1,), (1,)), ((), ())), preferred_element_type=jnp.float32
    ).reshape(batches, patterns_per, 2 * REACH + 1, count)
    scores = raw[:, :, REACH] * scale[:, :, None]
    best = top_values(scores)

    group_base = (section_index * orients + orient_index) * count
    local = best_picks - group_base
    owned = local[:, :, None] == lax.broadcasted_iota(jnp.int32, (batches, patterns_per, count), 2)
    picked = jnp.sum(jnp.where(owned[:, :, None], raw, 0.0), axis=3) * scale[:, :, None]
    packed = jnp.concatenate([best, picked], axis=-1)

    mine = lax.all_to_all(packed, "section", 0, 0, tiled=True)
    merged = merge_packed(mine, 0)
    everyone = lax.all_gather(merged, "orient", axis=0)
    final = merge_packed(everyone, 0)
    share = patterns_per // orients
    rows = lax.dynamic_slice_in_dim(final[:, TOPK:], orient_index * share, share, axis=0)
    return (final[None, :, :TOPK], rows[None])


def solution(mesh):
    return jax.shard_map(
        body,
        mesh=mesh,
        in_specs=(
            P("section", None, "orient"),
            P("orient"),
            P("orient"),
            P("orient"),
            P(("section", "orient"), None),
            P(),
        ),
        out_specs=(P("section", None, None), P("section", "orient", None)),
        check_vma=False,
    )
```

```python
import functools

import jax
import jax.numpy as jnp
from jax import lax
from jax.experimental import pallas as pl
from jax.experimental.pallas import tpu as pltpu
from jax.sharding import PartitionSpec as P

RAD = 64
ANG = 192
TOPK = 8
REACH = 1


EPS = 1e-06
BIN_BLOCK = 1024


def bin_kernel(pat_ref, bg_ref, gain_ref, map_ref, out_ref, corr_ref):
    step = pl.program_id(0)

    @pl.when(step == 0)
    def _():
        corr_ref[...] = (
            (pat_ref[...].astype(jnp.float32) - bg_ref[...]) * gain_ref[...]
        ).astype(jnp.bfloat16)

    height, width = out_ref.shape[0], map_ref.shape[1]
    targets = step * height + lax.broadcasted_iota(jnp.int32, (height, width), 0)
    onehot = (map_ref[...] == targets).astype(jnp.bfloat16)
    out_ref[...] = lax.dot_general(
        onehot, corr_ref[...], (((1,), (1,)), ((), ())), preferred_element_type=jnp.float32
    )


def bin_pixels(frames, background, gain, bin_map, total):
    rows, width = frames.shape
    height = min(BIN_BLOCK, total)
    full = lambda step: (0, 0)
    return pl.pallas_call(
        bin_kernel,
        grid=(total // height,),
        in_specs=[
            pl.BlockSpec((rows, width), full),
            pl.BlockSpec((1, width), full),
            pl.BlockSpec((1, width), full),
            pl.BlockSpec((1, width), full),
        ],
        out_specs=pl.BlockSpec((height, rows), lambda step: (step, 0)),
        out_shape=jax.ShapeDtypeStruct((total, rows), jnp.float32),
        scratch_shapes=[pltpu.VMEM((rows, width), jnp.bfloat16)],
        cost_estimate=pl.CostEstimate(
            flops=2 * total * width * rows, transcendentals=0,
            bytes_accessed=rows * width * 2 + total * rows * 4,
        ),
    )(frames, background[None, :], gain[None, :], bin_map[None, :])


def top_values(values):
    width = values.shape[-1]
    place = lax.broadcasted_iota(jnp.int32, values.shape, values.ndim - 1)
    found = []
    for rank in range(TOPK):
        largest = jnp.max(values, axis=-1, keepdims=True)
        found.append(largest)
        if rank + 1 < TOPK:
            first = jnp.min(jnp.where(values == largest, place, width), axis=-1, keepdims=True)
            values = jnp.where(place == first, -jnp.inf, values)
    return jnp.concatenate(found, axis=-1)


def merge_packed(stack, axis):
    best = jnp.moveaxis(stack[..., :TOPK], axis, -2)
    best = best.reshape(best.shape[:-2] + (best.shape[-2] * TOPK,))
    best = top_values(best)
    refined = jnp.sum(stack[..., TOPK:], axis=axis)
    return jnp.concatenate([best, refined], axis=-1)


def body(patterns, detector_gain, background, bin_map, templates, best_picks):
    sections = lax.axis_size("section")
    orients = lax.axis_size("orient")
    section_index = lax.axis_index("section")
    orient_index = lax.axis_index("orient")
    features_total = RAD * ANG
    batches, patterns_per = best_picks.shape
    count = templates.shape[0]

    bins = bin_pixels(patterns[0], background, detector_gain, bin_map, features_total)
    pieces = lax.all_to_all(bins.astype(jnp.bfloat16), "orient", 0, 0, tiled=True)
    part = jnp.sum(
        pieces.reshape(orients, features_total // orients, patterns_per).astype(jnp.float32), axis=0
    ).astype(jnp.bfloat16)
    gathered = lax.all_gather(
        part, ("section", "orient"), axis=0, tiled=True
    ).reshape(batches, features_total, patterns_per)

    squares = jnp.einsum(
        "mfp,mfp->mp", gathered, gathered, preferred_element_type=jnp.float32
    )
    scale = lax.rsqrt(squares / features_total + EPS)

    group_base = (section_index * orients + orient_index) * count
    local = best_picks - group_base
    owned = local[:, :, None] == lax.broadcasted_iota(jnp.int32, (batches, patterns_per, count), 2)
    chosen = jnp.einsum(
        "tf,mpt->mfp", templates, owned.astype(jnp.bfloat16), preferred_element_type=jnp.float32
    ).reshape(batches, RAD, ANG, patterns_per)
    rings = gathered.reshape(batches, RAD, ANG, patterns_per).astype(jnp.float32)
    columns = [
        jnp.sum(rings * jnp.roll(chosen, -offset, axis=2), axis=(1, 2))
        for offset in range(-REACH, REACH + 1)
    ]
    picked = jnp.stack(columns, axis=-1) * scale[:, :, None]

    raw = lax.dot_general(
        gathered, templates, (((1,), (1,)), ((), ())), preferred_element_type=jnp.float32
    )
    best = top_values(raw * scale[:, :, None])
    packed = jnp.concatenate([best, picked], axis=-1)

    mine = lax.all_to_all(packed, "section", 0, 0, tiled=True)
    merged = merge_packed(mine, 0)
    everyone = lax.all_gather(merged, "orient", axis=0)
    final = merge_packed(everyone, 0)
    share = patterns_per // orients
    rows = lax.dynamic_slice_in_dim(final[:, TOPK:], orient_index * share, share, axis=0)
    return (final[None, :, :TOPK], rows[None])


def solution(mesh):
    return jax.shard_map(
        body,
        mesh=mesh,
        in_specs=(
            P("section", None, "orient"),
            P("orient"),
            P("orient"),
            P("orient"),
            P(("section", "orient"), None),
            P(),
        ),
        out_specs=(P("section", None, None), P("section", "orient", None)),
        check_vma=False,
    )
```

```python
import functools

import jax
import jax.numpy as jnp
from jax import lax
from jax.experimental import pallas as pl
from jax.experimental.pallas import tpu as pltpu
from jax.sharding import PartitionSpec as P

RAD = 64
ANG = 192
TOPK = 8
REACH = 1


EPS = 1e-06
BIN_BLOCK = 1024


def bin_kernel(pat_ref, bg_ref, gain_ref, map_ref, out_ref, corr_ref):
    step = pl.program_id(0)

    @pl.when(step == 0)
    def _():
        corr_ref[...] = (
            (pat_ref[...].astype(jnp.float32) - bg_ref[...]) * gain_ref[...]
        ).astype(jnp.bfloat16)

    height, width = out_ref.shape[0], map_ref.shape[1]
    targets = step * height + lax.broadcasted_iota(jnp.int32, (height, width), 0)
    onehot = (map_ref[...] == targets).astype(jnp.bfloat16)
    out_ref[...] = lax.dot_general(
        onehot, corr_ref[...], (((1,), (1,)), ((), ())), preferred_element_type=jnp.float32
    )


def bin_pixels(frames, background, gain, bin_map, total):
    rows, width = frames.shape
    height = min(BIN_BLOCK, total)
    full = lambda step: (0, 0)
    return pl.pallas_call(
        bin_kernel,
        grid=(total // height,),
        in_specs=[
            pl.BlockSpec((rows, width), full),
            pl.BlockSpec((1, width), full),
            pl.BlockSpec((1, width), full),
            pl.BlockSpec((1, width), full),
        ],
        out_specs=pl.BlockSpec((height, rows), lambda step: (step, 0)),
        out_shape=jax.ShapeDtypeStruct((total, rows), jnp.float32),
        scratch_shapes=[pltpu.VMEM((rows, width), jnp.bfloat16)],
        cost_estimate=pl.CostEstimate(
            flops=2 * total * width * rows, transcendentals=0,
            bytes_accessed=rows * width * 2 + total * rows * 4,
        ),
    )(frames, background[None, :], gain[None, :], bin_map[None, :])


def top_values(values):
    width = values.shape[-1]
    place = lax.broadcasted_iota(jnp.int32, values.shape, values.ndim - 1)
    found = []
    for rank in range(TOPK):
        largest = jnp.max(values, axis=-1, keepdims=True)
        found.append(largest)
        if rank + 1 < TOPK:
            first = jnp.min(jnp.where(values == largest, place, width), axis=-1, keepdims=True)
            values = jnp.where(place == first, -jnp.inf, values)
    return jnp.concatenate(found, axis=-1)


def rotated_dot(rings, chosen, offset):
    width = rings.shape[2]
    spans = [(0, width)] if offset == 0 else (
        [(0, width - offset), (width - offset, width)] if offset > 0 else [(0, -offset), (-offset, width)]
    )
    total = 0.0
    for low, high in spans:
        near = lax.slice_in_dim(rings, low, high, axis=2).astype(jnp.float32)
        far_low = (low + offset) % width
        far = lax.slice_in_dim(chosen, far_low, far_low + high - low, axis=2).astype(jnp.float32)
        total = total + jnp.sum(near * far, axis=(1, 2))
    return total


def merge_packed(stack, axis):
    best = jnp.moveaxis(stack[..., :TOPK], axis, -2)
    best = best.reshape(best.shape[:-2] + (best.shape[-2] * TOPK,))
    best = top_values(best)
    refined = jnp.sum(stack[..., TOPK:], axis=axis)
    return jnp.concatenate([best, refined], axis=-1)


def body(patterns, detector_gain, background, bin_map, templates, best_picks):
    sections = lax.axis_size("section")
    orients = lax.axis_size("orient")
    section_index = lax.axis_index("section")
    orient_index = lax.axis_index("orient")
    features_total = RAD * ANG
    batches, patterns_per = best_picks.shape
    count = templates.shape[0]

    bins = bin_pixels(patterns[0], background, detector_gain, bin_map, features_total)
    pieces = lax.all_to_all(bins.astype(jnp.bfloat16), "orient", 0, 0, tiled=True)
    part = jnp.sum(
        pieces.reshape(orients, features_total // orients, patterns_per).astype(jnp.float32), axis=0
    ).astype(jnp.bfloat16)
    gathered = lax.all_gather(
        part, ("section", "orient"), axis=0, tiled=True
    ).reshape(batches, features_total, patterns_per)

    squares = jnp.einsum(
        "mfp,mfp->mp", gathered, gathered, preferred_element_type=jnp.float32
    )
    scale = lax.rsqrt(squares / features_total + EPS)

    group_base = (section_index * orients + orient_index) * count
    local = best_picks - group_base
    owned = local[:, :, None] == lax.broadcasted_iota(jnp.int32, (batches, patterns_per, count), 2)
    chosen = jnp.einsum(
        "tf,mpt->mfp", templates, owned.astype(jnp.bfloat16), preferred_element_type=jnp.float32
    ).astype(jnp.bfloat16)
    chosen = lax.optimization_barrier(chosen).reshape(batches, RAD, ANG, patterns_per)
    rings = gathered.reshape(batches, RAD, ANG, patterns_per)
    picked = jnp.stack(
        [rotated_dot(rings, chosen, offset) for offset in range(-REACH, REACH + 1)], axis=-1
    ) * scale[:, :, None]

    raw = lax.dot_general(
        gathered, templates, (((1,), (1,)), ((), ())), preferred_element_type=jnp.float32
    )
    best = top_values(raw * scale[:, :, None])
    packed = jnp.concatenate([best, picked], axis=-1)

    mine = lax.all_to_all(packed, "section", 0, 0, tiled=True)
    merged = merge_packed(mine, 0)
    everyone = lax.all_to_all(
        jnp.broadcast_to(merged[None], (orients,) + merged.shape), "orient", 0, 0
    )
    final = merge_packed(everyone, 0)
    share = patterns_per // orients
    rows = lax.dynamic_slice_in_dim(final[:, TOPK:], orient_index * share, share, axis=0)
    return (final[None, :, :TOPK], rows[None])


def solution(mesh):
    return jax.shard_map(
        body,
        mesh=mesh,
        in_specs=(
            P("section", None, "orient"),
            P("orient"),
            P("orient"),
            P("orient"),
            P(("section", "orient"), None),
            P(),
        ),
        out_specs=(P("section", None, None), P("section", "orient", None)),
        check_vma=False,
    )
```
